256 devices in a mesh: inner: 8 (over x, core), outer: 32 (over z, y).
Axes of the slice: x: 4, y: 4, z: 8, core: 2. Of those that a mesh axis runs over, the one named last changes fastest.
Arguments:
- queries: bfloat16 [32768, 2048], P(('outer', 'inner')), may hold values from -6 to 6
- keys: bfloat16 [32768, 2048], P(('outer', 'inner')), may hold values from -6 to 6
- values: bfloat16 [32768, 2048], P(('outer', 'inner')), may hold values from -6 to 6
- out_grad: bfloat16 [32768, 2048], P(('outer', 'inner')), may hold values from -6 to 6
- positions: int32 [32768], P(('outer', 'inner')), may hold values from 0 to 8191
Outputs:
- attended: bfloat16 [32768, 2048], P(('outer', 'inner'))
- query_grad: bfloat16 [32768, 2048], P(('outer', 'inner'))
- key_grad: bfloat16 [32768, 2048], P(('outer', 'inner'))
- value_gradient: bfloat16 [32768, 2048], P(('outer', 'inner'))
The draws below stay inside these ranges and needn't reach their ends.
All inputs are finite; a program needn't handle non-finite values.
Results may differ from the reference program's by a relative error of at most 0.0064.
Values sent between devices are 32-bit elements; how exact they have to be, the bound alone decides.
A program may use at most 256 MiB of HBM per device.

```python
import math
import jax
import jax.numpy as jnp
from jax import lax

HEADS = 16
D_HEAD = 128
TOK_DEV = 128
TOKENS = 32768


def plant(array, rng, low, largest):
    longest = array.shape.index(max(array.shape))
    spots = []
    for shift in (0, 1):
        where = [jax.random.randint(jax.random.fold_in(rng, axis), (), 0, length) for axis, length in enumerate(array.shape)]
        where[longest] = (where[longest] + shift) % array.shape[longest]
        spots.append(tuple(where))
    return array.at[spots[0]].set(low).at[spots[1]].set(largest)


def block_scale(rng, extent, shards, smallest, largest):
    level = 1.0
    for position, parts in shards:
        heights = jax.random.uniform(jax.random.fold_in(jax.random.fold_in(rng, 6), position), (parts,), jnp.float32, smallest / len(shards), largest / len(shards))
        level = level * jnp.repeat(jnp.exp(heights), extent[position] // parts).reshape((-1,) + (1,) * (len(extent) - 1 - position))
    return level


def scatter_about(own_key, extent, scale, most, cuts=(), dtype=jnp.bfloat16):
    result = scale * jax.random.normal(own_key, extent, jnp.float32)
    if cuts:
        result = result * block_scale(own_key, extent, cuts, -0.22, 0.18)
    return jnp.clip(result, -most, most).astype(dtype)


def setup_inputs(seed: int = 0) -> dict:
    seeds = jax.random.split(jax.random.key(seed), 6)
    queries = scatter_about(seeds[0], (TOKENS, HEADS * D_HEAD), 1.0, 6.0, ((0, 256),))
    keys = scatter_about(seeds[1], (TOKENS, HEADS * D_HEAD), 1.0, 6.0, ((0, 256),))
    values = scatter_about(seeds[2], (TOKENS, HEADS * D_HEAD), 1.0, 6.0, ((0, 256),))
    out_grad = scatter_about(seeds[3], (TOKENS, HEADS * D_HEAD), 1.0, 6.0, ((0, 256),))
    positions = plant(jax.random.randint(seeds[4], (TOKENS,), 0, 8192), jax.random.fold_in(seeds[4], 1), 0, 8191).astype(jnp.int32)
    return dict(queries=queries, keys=keys, values=values, out_grad=out_grad, positions=positions)


def rotary_tables(positions, head_dim):
    half_dim = head_dim // 2
    spacing = jnp.arange(half_dim).astype(jnp.float32) * (-2.0 * math.log(500000.0) / head_dim)
    angle = positions.astype(jnp.float32)[:, None] * jnp.exp(spacing)[None, :]
    return jnp.cos(angle)[:, None, :], jnp.sin(angle)[:, None, :]


def rotate(rows, cosine, sine):
    half_dim = rows.shape[-1] // 2
    first = rows[..., :half_dim].astype(jnp.float32)
    second = rows[..., half_dim:].astype(jnp.float32)
    return jnp.concatenate([first * cosine - second * sine, second * cosine + first * sine], axis=-1)


def unrotate(rows, cosine, sine):
    half_dim = rows.shape[-1] // 2
    first = rows[..., :half_dim]
    second = rows[..., half_dim:]
    return jnp.concatenate([first * cosine + second * sine, second * cosine - first * sine], axis=-1)


def block_state(pair):
    left_operand, right_operand = pair
    return jnp.einsum("pob,poj->obj", left_operand.astype(jnp.float32), right_operand.astype(jnp.float32))


def reference(queries, keys, values, out_grad, positions):
    scale_factor = (D_HEAD * TOKENS) ** -0.5
    blocks = TOKENS // TOK_DEV
    shaped = (blocks, TOK_DEV, HEADS, D_HEAD)
    cosine, sine = rotary_tables(positions, D_HEAD)
    rotated_query = rotate(queries.reshape(TOKENS, HEADS, D_HEAD), cosine, sine).astype(jnp.bfloat16).reshape(shaped)
    rotated_key = rotate(keys.reshape(TOKENS, HEADS, D_HEAD), cosine, sine).astype(jnp.bfloat16).reshape(shaped)
    value_row_block = values.reshape(shaped)
    gradient_row_block = out_grad.reshape(shaped)
    cos_blocks = cosine.reshape(blocks, TOK_DEV, 1, D_HEAD // 2)
    sin_blocks = sine.reshape(blocks, TOK_DEV, 1, D_HEAD // 2)
    key_value_state = lax.map(block_state, (rotated_key, value_row_block))
    query_state = lax.map(block_state, (rotated_query, gradient_row_block))
    preceding_state = (jnp.cumsum(key_value_state, axis=0) - key_value_state).astype(jnp.bfloat16)
    following_state = (jnp.cumsum(query_state[::-1], axis=0)[::-1] - query_state).astype(jnp.bfloat16)
    causal = jnp.arange(TOK_DEV)[:, None] >= jnp.arange(TOK_DEV)[None, :]

    def one_block(items):
        qrot, krot, vrow, grow, cosb, sinb, before, after = items
        query_float = qrot.astype(jnp.float32)
        key_float = krot.astype(jnp.float32)
        value_float = vrow.astype(jnp.float32)
        gradient_float = grow.astype(jnp.float32)
        second_operand = before.astype(jnp.float32)
        first_operand = after.astype(jnp.float32)
        score_matrix = jnp.where(causal[None], jnp.einsum("thd,shd->hts", query_float, key_float), 0.0).astype(jnp.bfloat16).astype(jnp.float32)
        score_gradient = jnp.where(causal[None], jnp.einsum("thd,shd->hts", gradient_float, value_float), 0.0).astype(jnp.bfloat16).astype(jnp.float32)
        attended = scale_factor * (jnp.einsum("rgb,brf->grf", score_matrix, value_float) + jnp.einsum("axz,xzo->axo", query_float, second_operand))
        rotated_query_gradient = scale_factor * (jnp.einsum("rgb,brf->grf", score_gradient, key_float) + jnp.einsum("xge,gme->xgm", gradient_float, second_operand))
        rotated_key_gradient = scale_factor * (jnp.einsum("uox,oul->xul", score_gradient, query_float) + jnp.einsum("olb,lfb->olf", value_float, first_operand))
        value_gradient = scale_factor * (jnp.einsum("uox,oul->xul", score_matrix, gradient_float) + jnp.einsum("tyg,yge->tye", key_float, first_operand))
        return (attended.astype(jnp.bfloat16), unrotate(rotated_query_gradient, cosb, sinb).astype(jnp.bfloat16),
                unrotate(rotated_key_gradient, cosb, sinb).astype(jnp.bfloat16), value_gradient.astype(jnp.bfloat16))

    results = lax.map(one_block, (rotated_query, rotated_key, value_row_block, gradient_row_block, cos_blocks, sin_blocks, preceding_state, following_state))
    flat = (TOKENS, HEADS * D_HEAD)
    return (results[0].reshape(flat), results[1].reshape(flat), results[2].reshape(flat), results[3].reshape(flat))
```

```python
import functools
import math

import jax
import jax.numpy as jnp
from jax import lax
from jax.experimental import pallas as pl
from jax.experimental.pallas import tpu as pltpu
from jax.sharding import PartitionSpec as P

D_HEAD = 128
CORES = 2
F32, BF16 = (jnp.float32, jnp.bfloat16)


def rotate(rows, cosine, sine):
    rows = rows.astype(F32)
    return rows * cosine + pltpu.roll(rows, D_HEAD // 2, 1) * sine


def unrotate(rows, cosine, sine):
    return rows * cosine - pltpu.roll(rows, D_HEAD // 2, 1) * sine


def dot(left, right, left_dim, right_dim):
    return lax.dot_general(
        left, right, (((left_dim,), (right_dim,)), ((), ())), preferred_element_type=F32
    )


def columns(head):
    return pl.ds(pl.multiple_of(head * D_HEAD, D_HEAD), D_HEAD)


def scan_kernel(
    sizes,
    q_ref, k_ref, v_ref, g_ref, cos_ref, sin_ref,
    before_ref, after_ref,
    theirs, own, pin, chip, xin, row, yin, plane, zin, yout, ybase, xout, xbase, pout, pbase,
    core_s, core_r, x_s, x_r, y_s, y_r, z_s, z_r, yb_s, yb_r, xb_s, xb_r, cb_s, cb_r,
):
    nx, ny, nz, per = sizes
    inner, outer = (lax.axis_index("inner"), lax.axis_index("outer"))
    x, c = (inner // CORES, lax.rem(inner, CORES))
    z, y = (outer // ny, lax.rem(outer, ny))
    part = D_HEAD // ny
    other = 1 - c

    def at(xx, cc, yy, zz):
        return {"inner": xx * CORES + cc, "outer": zz * ny + yy}

    def shifted(place, by, count):
        return lax.rem(place + by, count)

    partner = at(x, other, y, z)
    x_dev = [at(shifted(x, d, nx), c, y, z) for d in range(nx)]
    y_dev = [at(x, c, shifted(y, d, ny), z) for d in range(ny)]
    z_dev = [at(x, c, y, shifted(z, d, nz)) for d in range(nz)]
    barrier = pltpu.get_barrier_semaphore()
    peers = [partner] + x_dev[1:] + y_dev[1:] + z_dev[1:]
    for peer in peers:
        pl.semaphore_signal(barrier, inc=1, device_id=peer, device_id_type=pl.DeviceIdType.MESH)

    sent = []

    def remote(src, dst, send, recv, device):
        return pltpu.make_async_remote_copy(
            src_ref=src, dst_ref=dst, send_sem=send, recv_sem=recv,
            device_id=device, device_id_type=pl.DeviceIdType.MESH,
        )

    def post(*args):
        copy = remote(*args)
        copy.start()
        sent.append(copy)

    cosine, sine = (cos_ref[...], sin_ref[...])
    far_first = sorted(range(nx), key=lambda d: (d == 0, -min(d, nx - d)))

    def states(head, put):
        at_head = columns(head)
        key = rotate(k_ref[:, at_head], cosine, sine).astype(BF16)
        put[0] = dot(key, v_ref[:, at_head], 0, 0)
        query = rotate(q_ref[:, at_head], cosine, sine).astype(BF16)
        put[1] = dot(query, g_ref[:, at_head], 0, 0)

    def head_of(xx, cc, j):
        return (xx * CORES + cc) * per + j

    first = True
    for j in range(per):
        for d in far_first:
            xx = shifted(x, d, nx)
            states(head_of(xx, other, j), theirs.at[xx, j])
            if first:
                pl.semaphore_wait(barrier, len(peers))
                first = False
            post(theirs.at[xx, j], pin.at[xx, j], core_s.at[d, j], core_r.at[d, j], partner)
    for j in range(per):
        for d in far_first:
            xx = shifted(x, d, nx)
            states(head_of(xx, c, j), own.at[xx, j])

    for j in range(per):
        for d in far_first:
            xx = shifted(x, d, nx)
            remote(theirs.at[xx, j], pin.at[xx, j], core_s.at[d, j], core_r.at[d, j], partner).wait_recv()
            if d:
                chip[xx, j] = own[xx, j] + pin[xx, j]
                post(chip.at[xx, j], xin.at[x, j], x_s.at[d, j], x_r.at[d, j], x_dev[d])
            else:
                xin[x, j] = own[x, j] + pin[x, j]

    for j in range(per):
        for d in range(1, nx):
            src = shifted(x, nx - d, nx)
            remote(chip.at[src, j], xin.at[src, j], x_s.at[d, j], x_r.at[d, j], x_dev[d]).wait_recv()
        total = xin[0, j]
        for xx in range(1, nx):
            total = total + xin[xx, j]
        row[j] = total
        for d in range(1, ny):
            rows = pl.ds(pl.multiple_of(shifted(y, d, ny) * part, part), part)
            post(row.at[j, :, rows], yin.at[y, j], y_s.at[d, j], y_r.at[d, j], y_dev[d])
        yin[y, j] = row[j, :, pl.ds(pl.multiple_of(y * part, part), part)]

    for j in range(per):
        for d in range(1, ny):
            src = shifted(y, ny - d, ny)
            remote(yout.at[src, j], yin.at[src, j], y_s.at[d, j], y_r.at[d, j], y_dev[d]).wait_recv()
        total = yin[0, j]
        for yy in range(1, ny):
            total = total + yin[yy, j]
        plane[j] = total
        for d in range(1, nz):
            which = jnp.where(z + d >= nz, 1, 0)
            post(plane.at[j, which], zin.at[z, j], z_s.at[d, j], z_r.at[d, j], z_dev[d])
        zin[z, j] = jnp.zeros((part, D_HEAD), F32)

    for j in range(per):
        for d in range(1, nz):
            src = shifted(z, nz - d, nz)
            remote(plane.at[j, 0], zin.at[src, j], z_s.at[d, j], z_r.at[d, j], z_dev[d]).wait_recv()
        earlier = jnp.zeros((part, D_HEAD), F32)
        later = jnp.zeros((part, D_HEAD), F32)
        for zz in range(nz):
            piece = zin[zz, j]
            earlier = earlier + jnp.where(zz < z, piece, 0.0)
            later = later + jnp.where(zz > z, piece, 0.0)
        for yy in range(ny):
            yout[yy, j, 0] = earlier
            earlier = earlier + yin[yy, j, 0]
        for yy in reversed(range(ny)):
            yout[yy, j, 1] = later
            later = later + yin[yy, j, 1]
        mine = pl.ds(pl.multiple_of(y * part, part), part)
        for d in range(1, ny):
            yy = shifted(y, d, ny)
            post(yout.at[yy, j], ybase.at[j, :, mine], yb_s.at[d, j], yb_r.at[d, j], y_dev[d])
        ybase[j, :, mine] = yout[y, j]

    for j in range(per):
        for d in range(1, ny):
            src = shifted(y, ny - d, ny)
            rows = pl.ds(pl.multiple_of(src * part, part), part)
            remote(yout.at[src, j], ybase.at[j, :, rows], yb_s.at[d, j], yb_r.at[d, j], y_dev[d]).wait_recv()
        earlier = ybase[j, 0]
        for xx in range(nx):
            xout[xx, j, 0] = earlier
            earlier = earlier + xin[xx, j, 0]
        later = ybase[j, 1]
        for xx in reversed(range(nx)):
            xout[xx, j, 1] = later
            later = later + xin[xx, j, 1]
        for d in far_first:
            xx = shifted(x, d, nx)
            if d:
                post(xout.at[xx, j], xbase.at[x, j], xb_s.at[d, j], xb_r.at[d, j], x_dev[d])
            else:
                xbase[x, j] = xout[x, j]

    for j in range(per):
        for d in reversed(far_first):
            src = shifted(x, nx - d, nx)
            if d:
                remote(xout.at[src, j], xbase.at[src, j], xb_s.at[d, j], xb_r.at[d, j], x_dev[d]).wait_recv()
            keys, queries = (xbase[src, j, 0], xbase[src, j, 1])
            pout[src, j, 0] = keys + jnp.where(c == 0, own[src, j, 0], 0.0)
            pout[src, j, 1] = queries + jnp.where(c == 1, own[src, j, 1], 0.0)
            post(pout.at[src, j], pbase.at[src, j], cb_s.at[d, j], cb_r.at[d, j], partner)
            head = head_of(src, c, j)
            before_ref[head] = (keys + jnp.where(c == 1, pin[src, j, 0], 0.0)).astype(BF16)
            after_ref[head] = (queries + jnp.where(c == 0, pin[src, j, 1], 0.0)).astype(BF16)

    for j in range(per):
        for d in reversed(far_first):
            src = shifted(x, nx - d, nx)
            remote(pout.at[src, j], pbase.at[src, j], cb_s.at[d, j], cb_r.at[d, j], partner).wait_recv()
            head = head_of(src, other, j)
            before_ref[head] = pbase[src, j, 0].astype(BF16)
            after_ref[head] = pbase[src, j, 1].astype(BF16)
    for copy in sent:
        copy.wait_send()


def block_kernel(
    scale, heads, q_ref, k_ref, v_ref, g_ref, cos_ref, sin_ref, before_ref, after_ref,
    attended_ref, query_grad_ref, key_grad_ref, value_grad_ref,
):
    cosine, sine = (cos_ref[...], sin_ref[...])
    tokens = q_ref.shape[0]
    causal = lax.broadcasted_iota(jnp.int32, (tokens, tokens), 0) >= lax.broadcasted_iota(
        jnp.int32, (tokens, tokens), 1
    )
    for n in range(heads):
        cols = slice(n * D_HEAD, (n + 1) * D_HEAD)
        query = rotate(q_ref[:, cols], cosine, sine).astype(BF16)
        key = rotate(k_ref[:, cols], cosine, sine).astype(BF16)
        value, grad = (v_ref[:, cols], g_ref[:, cols])
        before, after = (before_ref[n], after_ref[n])
        scores = jnp.where(causal, dot(query, key, 1, 1), 0.0).astype(BF16)
        grad_scores = jnp.where(causal, dot(grad, value, 1, 1), 0.0).astype(BF16)
        attended = dot(scores, value, 1, 0) + dot(query, before, 1, 0)
        attended_ref[:, cols] = (scale * attended).astype(BF16)
        query_grad = scale * (dot(grad_scores, key, 1, 0) + dot(grad, before, 1, 1))
        query_grad_ref[:, cols] = unrotate(query_grad, cosine, sine).astype(BF16)
        key_grad = scale * (dot(grad_scores, query, 0, 0) + dot(value, after, 1, 1))
        key_grad_ref[:, cols] = unrotate(key_grad, cosine, sine).astype(BF16)
        value_grad = scale * (dot(scores, grad, 0, 0) + dot(key, after, 1, 0))
        value_grad_ref[:, cols] = value_grad.astype(BF16)


def shards(sizes, queries, keys, values, out_grad, positions):
    nx, ny, nz, per = sizes
    tokens, width = queries.shape
    heads = width // D_HEAD
    total_tokens = tokens * lax.axis_size("inner") * lax.axis_size("outer")
    scale = (D_HEAD * total_tokens) ** (-0.5)
    half = D_HEAD // 2
    spacing = jnp.arange(half).astype(F32) * (-2.0 * math.log(500000.0) / D_HEAD)
    angle = positions.astype(F32)[:, None] * jnp.exp(spacing)[None, :]
    cosine, sine = (jnp.cos(angle), jnp.sin(angle))
    cosine = jnp.concatenate([cosine, cosine], axis=1)
    sine = jnp.concatenate([-sine, sine], axis=1)

    part = D_HEAD // ny
    square = (per, 2, D_HEAD, D_HEAD)
    by_x = pltpu.VMEM((nx,) + square, F32)
    by_y = pltpu.VMEM((ny, per, 2, part, D_HEAD), F32)
    whole = pl.BlockSpec(memory_space=pltpu.VMEM)
    sems = []
    for count in (nx, nx, ny, nz, ny, nx, nx):
        sems += [pltpu.SemaphoreType.DMA((count, per))] * 2
    before, after = pl.pallas_call(
        functools.partial(scan_kernel, sizes),
        out_shape=[jax.ShapeDtypeStruct((heads, D_HEAD, D_HEAD), BF16)] * 2,
        in_specs=[whole] * 6,
        out_specs=[whole] * 2,
        scratch_shapes=[
            by_x, by_x, by_x, by_x, by_x,
            pltpu.VMEM(square, F32),
            by_y,
            pltpu.VMEM((per, 2, part, D_HEAD), F32),
            pltpu.VMEM((nz, per, part, D_HEAD), F32),
            by_y,
            pltpu.VMEM(square, F32),
            by_x, by_x, by_x, by_x,
        ] + sems,
        compiler_params=pltpu.CompilerParams(
            collective_id=0, has_side_effects=True, vmem_limit_bytes=48 * 1024 * 1024
        ),
        name="scan",
    )(queries, keys, values, out_grad, cosine, sine)

    at_once = 4
    rows = pl.BlockSpec((tokens, at_once * D_HEAD), lambda n: (0, n))
    table = pl.BlockSpec((tokens, D_HEAD), lambda n: (0, 0))
    state = pl.BlockSpec((at_once, D_HEAD, D_HEAD), lambda n: (n, 0, 0))
    return pl.pallas_call(
        functools.partial(block_kernel, scale, at_once),
        grid=(heads // at_once,),
        out_shape=[jax.ShapeDtypeStruct((tokens, width), BF16)] * 4,
        in_specs=[rows] * 4 + [table] * 2 + [state] * 2,
        out_specs=[rows] * 4,
        name="block",
    )(queries, keys, values, out_grad, cosine, sine, before, after)


def solution(mesh):
    inner, outer = (mesh.shape["inner"], mesh.shape["outer"])
    ny = 4 if outer % 16 == 0 else 2
    sizes = (inner // CORES, ny, outer // ny, 16 // inner)
    both = P(("outer", "inner"), None)
    return jax.shard_map(
        functools.partial(shards, sizes),
        mesh=mesh,
        in_specs=(both,) * 4 + (P(("outer", "inner")),),
        out_specs=(both,) * 4,
        check_vma=False,
    )
```

```python
import functools
import math

import jax
import jax.numpy as jnp
from jax import lax
from jax.experimental import pallas as pl
from jax.experimental.pallas import tpu as pltpu
from jax.sharding import PartitionSpec as P

D_HEAD = 128
CORES = 2
HALVES = 2
F32, BF16 = (jnp.float32, jnp.bfloat16)


def rotate(rows, cosine, sine):
    rows = rows.astype(F32)
    return rows * cosine + pltpu.roll(rows, D_HEAD // 2, 1) * sine


def unrotate(rows, cosine, sine):
    return rows * cosine - pltpu.roll(rows, D_HEAD // 2, 1) * sine


def dot(left, right, left_dim, right_dim):
    return lax.dot_general(
        left, right, (((left_dim,), (right_dim,)), ((), ())), preferred_element_type=F32
    )


def columns(head, width=D_HEAD):
    return pl.ds(pl.multiple_of(head * width, width), width)


def scan_kernel(
    sizes, scale,
    q_hbm, k_hbm, v_hbm, g_hbm, pos_hbm,
    attended_ref, query_grad_ref, key_grad_ref, value_grad_ref,
    q_ref, k_ref, v_ref, g_ref, pos_ref, cos_ref, sin_ref, qrot, krot, partial, before, after,
    theirs, own, pin, chip, xin, row, yin, plane, zin, yout, ybase, xout, xbase, pout, pbase,
    in_s, pos_s, core_s, core_r, x_s, x_r, y_s, y_r, z_s, z_r, yb_s, yb_r, xb_s, xb_r, cb_s, cb_r,
):
    nx, ny, nz, per = sizes
    inner, outer = (lax.axis_index("inner"), lax.axis_index("outer"))
    x, c = (inner // CORES, lax.rem(inner, CORES))
    z, y = (outer // ny, lax.rem(outer, ny))
    tall = D_HEAD // HALVES
    part = tall // ny
    other = 1 - c
    tokens = q_ref.shape[0]

    def at(xx, cc, yy, zz):
        return {"inner": xx * CORES + cc, "outer": zz * ny + yy}

    def shifted(place, by, count):
        return lax.rem(place + by, count)

    partner = at(x, other, y, z)
    x_dev = [at(shifted(x, d, nx), c, y, z) for d in range(nx)]
    y_dev = [at(x, c, shifted(y, d, ny), z) for d in range(ny)]
    z_dev = [at(x, c, y, shifted(z, d, nz)) for d in range(nz)]
    barrier = pltpu.get_barrier_semaphore()
    peers = [partner] + x_dev[1:] + y_dev[1:] + z_dev[1:]
    for peer in peers:
        pl.semaphore_signal(barrier, inc=1, device_id=peer, device_id_type=pl.DeviceIdType.MESH)

    far_first = sorted(range(nx), key=lambda d: (d == 0, -min(d, nx - d)))
    near_first = far_first[::-1]
    arrays = ((k_hbm, k_ref), (v_hbm, v_ref), (q_hbm, q_ref), (g_hbm, g_ref))

    def fetch(side, d):
        cols = columns(shifted(x, d, nx) * CORES + (c if side else other), per * D_HEAD)
        return [
            pltpu.make_async_copy(src.at[:, cols], dst.at[:, cols], in_s.at[n, side, d])
            for n, (src, dst) in enumerate(arrays)
        ]

    place = pltpu.make_async_copy(pos_hbm, pos_ref, pos_s)
    place.start()
    for side in (0, 1):
        for d in far_first:
            for copy in fetch(side, d):
                copy.start()

    sent = []

    def remote(src, dst, send, recv, device):
        return pltpu.make_async_remote_copy(
            src_ref=src, dst_ref=dst, send_sem=send, recv_sem=recv,
            device_id=device, device_id_type=pl.DeviceIdType.MESH,
        )

    def post(*args):
        copy = remote(*args)
        copy.start()
        sent.append(copy)

    place.wait()
    half = D_HEAD // 2
    pair = lax.broadcasted_iota(jnp.int32, (half, tokens), 0).astype(F32)
    angle = pos_ref[...].astype(F32) * jnp.exp(pair * (-2.0 * math.log(500000.0) / D_HEAD))
    cosine, sine = (jnp.cos(angle), jnp.sin(angle))
    cos_ref[...] = jnp.concatenate([cosine, cosine], axis=0).T
    sin_ref[...] = jnp.concatenate([-sine, sine], axis=0).T

    def head_of(xx, cc, j):
        return (xx * CORES + cc) * per + j

    def states(head, put):
        cols = columns(head)
        cosine, sine = (cos_ref[...], sin_ref[...])
        key = rotate(k_ref[:, cols], cosine, sine).astype(BF16)
        krot[:, cols] = key
        put[0] = dot(key, v_ref[:, cols], 0, 0)
        query = rotate(q_ref[:, cols], cosine, sine).astype(BF16)
        qrot[:, cols] = query
        put[1] = dot(query, g_ref[:, cols], 0, 0)

    def in_block(head):
        cols = columns(head)
        query, key, value, grad = (qrot[:, cols], krot[:, cols], v_ref[:, cols], g_ref[:, cols])
        causal = lax.broadcasted_iota(jnp.int32, (tokens, tokens), 0) >= lax.broadcasted_iota(
            jnp.int32, (tokens, tokens), 1
        )
        scores = jnp.where(causal, dot(query, key, 1, 1), 0.0).astype(BF16)
        grad_scores = jnp.where(causal, dot(grad, value, 1, 1), 0.0).astype(BF16)
        partial[0, :, cols] = dot(scores, value, 1, 0)
        partial[1, :, cols] = dot(grad_scores, key, 1, 0)
        partial[2, :, cols] = dot(grad_scores, query, 0, 0)
        partial[3, :, cols] = dot(scores, grad, 0, 0)

    def finish(head):
        cols = columns(head)
        cosine, sine = (cos_ref[...], sin_ref[...])
        first, last = (before[head], after[head])
        attended = partial[0, :, cols] + dot(qrot[:, cols], first, 1, 0)
        attended_ref[:, cols] = (scale * attended).astype(BF16)
        query_grad = scale * (partial[1, :, cols] + dot(g_ref[:, cols], first, 1, 1))
        query_grad_ref[:, cols] = unrotate(query_grad, cosine, sine).astype(BF16)
        key_grad = scale * (partial[2, :, cols] + dot(v_ref[:, cols], last, 1, 1))
        key_grad_ref[:, cols] = unrotate(key_grad, cosine, sine).astype(BF16)
        value_grad = scale * (partial[3, :, cols] + dot(krot[:, cols], last, 1, 0))
        value_grad_ref[:, cols] = value_grad.astype(BF16)

    def spans(n):
        return n // HALVES, pl.ds((n % HALVES) * tall, tall)

    def start_states(j):
        for d in far_first:
            xx = shifted(x, d, nx)
            if j == 0:
                for copy in fetch(0, d):
                    copy.wait()
            states(head_of(xx, other, j), theirs.at[xx, j])
            if j == 0 and d == far_first[0]:
                pl.semaphore_wait(barrier, len(peers))
            post(theirs.at[xx, j], pin.at[xx, j], core_s.at[d, j], core_r.at[d, j], partner)
        for d in far_first:
            xx = shifted(x, d, nx)
            if j == 0:
                for copy in fetch(1, d):
                    copy.wait()
            states(head_of(xx, c, j), own.at[xx, j])

    def send_x(j):
        for d in far_first:
            xx = shifted(x, d, nx)
            remote(theirs.at[xx, j], pin.at[xx, j], core_s.at[d, j], core_r.at[d, j], partner).wait_recv()
            if d:
                chip[xx, j] = own[xx, j] + pin[xx, j]
            else:
                xin[x, j] = own[x, j] + pin[x, j]
        for n in range(j * HALVES, (j + 1) * HALVES):
            rows = spans(n)[1]
            for d in far_first[:-1]:
                xx = shifted(x, d, nx)
                post(chip.at[xx, j, :, rows], xin.at[x, j, :, rows], x_s.at[d, n], x_r.at[d, n], x_dev[d])

    def got_x(n):
        j, rows = spans(n)
        for d in range(1, nx):
            src = shifted(x, nx - d, nx)
            remote(chip.at[src, j, :, rows], xin.at[src, j, :, rows], x_s.at[d, n], x_r.at[d, n], x_dev[d]).wait_recv()
        total = xin[0, j, :, rows]
        for xx in range(1, nx):
            total = total + xin[xx, j, :, rows]
        row[n] = total
        for d in range(1, ny):
            cut = pl.ds(pl.multiple_of(shifted(y, d, ny) * part, part), part)
            post(row.at[n, :, cut], yin.at[y, n], y_s.at[d, n], y_r.at[d, n], y_dev[d])
        yin[y, n] = row[n, :, pl.ds(pl.multiple_of(y * part, part), part)]

    def got_y(n):
        for d in range(1, ny):
            src = shifted(y, ny - d, ny)
            remote(yout.at[src, n], yin.at[src, n], y_s.at[d, n], y_r.at[d, n], y_dev[d]).wait_recv()
        total = yin[0, n]
        for yy in range(1, ny):
            total = total + yin[yy, n]
        plane[n] = total
        for d in sorted(range(1, nz), key=lambda d: -min(d, nz - d)):
            which = jnp.where(z + d >= nz, 1, 0)
            post(plane.at[n, which], zin.at[z, n], z_s.at[d, n], z_r.at[d, n], z_dev[d])
        zin[z, n] = jnp.zeros((part, D_HEAD), F32)

    def got_z(n):
        for d in range(1, nz):
            src = shifted(z, nz - d, nz)
            remote(plane.at[n, 0], zin.at[src, n], z_s.at[d, n], z_r.at[d, n], z_dev[d]).wait_recv()
        earlier = jnp.zeros((part, D_HEAD), F32)
        later = jnp.zeros((part, D_HEAD), F32)
        for zz in range(nz):
            piece = zin[zz, n]
            earlier = earlier + jnp.where(zz < z, piece, 0.0)
            later = later + jnp.where(zz > z, piece, 0.0)
        for yy in range(ny):
            yout[yy, n, 0] = earlier
            earlier = earlier + yin[yy, n, 0]
        for yy in reversed(range(ny)):
            yout[yy, n, 1] = later
            later = later + yin[yy, n, 1]
        mine = pl.ds(pl.multiple_of(y * part, part), part)
        for d in range(1, ny):
            yy = shifted(y, d, ny)
            post(yout.at[yy, n], ybase.at[n, :, mine], yb_s.at[d, n], yb_r.at[d, n], y_dev[d])
        ybase[n, :, mine] = yout[y, n]

    def got_yb(n):
        j, rows = spans(n)
        for d in range(1, ny):
            src = shifted(y, ny - d, ny)
            cut = pl.ds(pl.multiple_of(src * part, part), part)
            remote(yout.at[src, n], ybase.at[n, :, cut], yb_s.at[d, n], yb_r.at[d, n], y_dev[d]).wait_recv()
        earlier = ybase[n, 0]
        for xx in range(nx):
            xout[xx, n, 0] = earlier
            earlier = earlier + xin[xx, j, 0, rows]
        later = ybase[n, 1]
        for xx in reversed(range(nx)):
            xout[xx, n, 1] = later
            later = later + xin[xx, j, 1, rows]
        for d in far_first[:-1]:
            xx = shifted(x, d, nx)
            post(xout.at[xx, n], xbase.at[x, n], xb_s.at[d, n], xb_r.at[d, n], x_dev[d])
        xbase[x, n] = xout[x, n]

    def got_xb(n):
        j, rows = spans(n)
        for d in near_first:
            src = shifted(x, nx - d, nx)
            if d:
                remote(xout.at[src, n], xbase.at[src, n], xb_s.at[d, n], xb_r.at[d, n], x_dev[d]).wait_recv()
            keys, queries = (xbase[src, n, 0], xbase[src, n, 1])
            pout[src, n, 0] = keys + jnp.where(c == 0, own[src, j, 0, rows], 0.0)
            pout[src, n, 1] = queries + jnp.where(c == 1, own[src, j, 1, rows], 0.0)
            post(pout.at[src, n], pbase.at[src, n], cb_s.at[d, n], cb_r.at[d, n], partner)
            head = head_of(src, c, j)
            before[head, rows] = (keys + jnp.where(c == 1, pin[src, j, 0, rows], 0.0)).astype(BF16)
            after[head, rows] = (queries + jnp.where(c == 0, pin[src, j, 1, rows], 0.0)).astype(BF16)

    def got_cb(n):
        j, rows = spans(n)
        for d in near_first:
            src = shifted(x, nx - d, nx)
            remote(pout.at[src, n], pbase.at[src, n], cb_s.at[d, n], cb_r.at[d, n], partner).wait_recv()
            head = head_of(src, other, j)
            before[head, rows] = pbase[src, n, 0].astype(BF16)
            after[head, rows] = pbase[src, n, 1].astype(BF16)

    def finish_side(j, cc):
        for d in near_first:
            finish(head_of(shifted(x, nx - d, nx), cc, j))

    heads = iter(range(nx * CORES * per))

    def some_heads(count):
        for _ in range(count):
            head = next(heads, None)
            if head is not None:
                in_block(head)

    chunks = per * HALVES
    for j in range(per):
        start_states(j)
        send_x(j)
    some_heads(5)
    stages = ((got_x, 0.0), (got_y, 3.1), (got_z, 8.4), (got_yb, 11.5), (got_xb, 16.7))
    events = sorted(
        (lag + 2.8 * 4 / chunks * n, k, n) for k, (_, lag) in enumerate(stages) for n in range(chunks)
    )
    for _, k, n in events:
        stages[k][0](n)
        if k < 2:
            some_heads(2)
        if k == 3 and n == chunks - 1:
            some_heads(nx * CORES * per)
            for j in range(per - 1):
                for m in range(j * HALVES, (j + 1) * HALVES):
                    got_cb(m)
                finish_side(j, c)
                finish_side(j, other)
    finish_side(per - 1, c)
    for n in range((per - 1) * HALVES, chunks):
        got_cb(n)
    finish_side(per - 1, other)
    for copy in sent:
        copy.wait_send()


def write_kernel(*refs):
    count = len(refs) // 2
    sem = refs[-1]
    copies = [pltpu.make_async_copy(refs[n], refs[count + n], sem.at[n]) for n in range(count)]
    for copy in copies:
        copy.start()
    for copy in copies:
        copy.wait()


def shards(sizes, queries, keys, values, out_grad, positions):
    nx, ny, nz, per = sizes
    tokens, width = queries.shape
    heads = width // D_HEAD
    total_tokens = tokens * lax.axis_size("inner") * lax.axis_size("outer")
    scale = (D_HEAD * total_tokens) ** (-0.5)
    chunks = per * HALVES
    tall = D_HEAD // HALVES
    part = tall // ny

    tokens_bf16 = pltpu.VMEM((tokens, width), BF16)
    table = pltpu.VMEM((tokens, D_HEAD), F32)
    state = pltpu.VMEM((heads, D_HEAD, D_HEAD), BF16)
    by_x = pltpu.VMEM((nx, per, 2, D_HEAD, D_HEAD), F32)
    by_x_chunk = pltpu.VMEM((nx, chunks, 2, tall, D_HEAD), F32)
    by_y = pltpu.VMEM((ny, chunks, 2, part, D_HEAD), F32)
    mine = pltpu.VMEM((chunks, 2, tall, D_HEAD), F32)
    in_vmem = pl.BlockSpec(memory_space=pltpu.VMEM)
    in_hbm = pl.BlockSpec(memory_space=pltpu.HBM)
    sems = [pltpu.SemaphoreType.DMA((4, 2, nx)), pltpu.SemaphoreType.DMA]
    for count in ((nx, per), (nx, chunks), (ny, chunks), (nz, chunks), (ny, chunks), (nx, chunks), (nx, chunks)):
        sems += [pltpu.SemaphoreType.DMA(count)] * 2
    results = [jax.ShapeDtypeStruct((tokens, width), BF16)] * 4
    arrays = (queries, keys, values, out_grad, positions.reshape(1, tokens))
    arrays = [pltpu.with_memory_space_constraint(a, pltpu.HBM) for a in arrays]
    outputs = pl.pallas_call(
        functools.partial(scan_kernel, sizes, scale),
        out_shape=[pltpu.VMEM((tokens, width), BF16)] * 4,
        in_specs=[in_hbm] * 5,
        out_specs=[in_vmem] * 4,
        scratch_shapes=[tokens_bf16] * 4 + [pltpu.VMEM((1, tokens), jnp.int32)] + [table] * 2 + [tokens_bf16] * 2
        + [pltpu.VMEM((4, tokens, width), F32), state, state]
        + [by_x] * 5 + [mine, by_y]
        + [pltpu.VMEM((chunks, 2, part, D_HEAD), F32), pltpu.VMEM((nz, chunks, part, D_HEAD), F32)]
        + [by_y, mine] + [by_x_chunk] * 4 + sems,
        compiler_params=pltpu.CompilerParams(
            collective_id=0, has_side_effects=True, vmem_limit_bytes=48 * 1024 * 1024
        ),
        name="scan",
    )(*arrays)
    return pl.pallas_call(
        write_kernel,
        out_shape=results,
        in_specs=[in_vmem] * 4,
        out_specs=[in_hbm] * 4,
        scratch_shapes=[pltpu.SemaphoreType.DMA((4,))],
        name="write",
    )(*[pltpu.with_memory_space_constraint(a, pltpu.VMEM) for a in outputs])


def solution(mesh):
    inner, outer = (mesh.shape["inner"], mesh.shape["outer"])
    ny = 4 if outer % 16 == 0 else 2
    sizes = (inner // CORES, ny, outer // ny, 16 // inner)
    both = P(("outer", "inner"), None)
    return jax.shard_map(
        functools.partial(shards, sizes),
        mesh=mesh,
        in_specs=(both,) * 4 + (P(("outer", "inner")),),
        out_specs=(both,) * 4,
        check_vma=False,
    )
```

```python
import functools
import math

import jax
import jax.numpy as jnp
from jax import lax
from jax.experimental import pallas as pl
from jax.experimental.pallas import tpu as pltpu
from jax.sharding import PartitionSpec as P

D_HEAD = 128
CORES = 2
HALVES = 2
F32, BF16 = (jnp.float32, jnp.bfloat16)


def rotate(rows, cosine, sine):
    rows = rows.astype(F32)
    return rows * cosine + pltpu.roll(rows, D_HEAD // 2, 1) * sine


def unrotate(rows, cosine, sine):
    return rows * cosine - pltpu.roll(rows, D_HEAD // 2, 1) * sine


def dot(left, right, left_dim, right_dim):
    return lax.dot_general(
        left, right, (((left_dim,), (right_dim,)), ((), ())), preferred_element_type=F32
    )


def columns(head, width=D_HEAD):
    return pl.ds(pl.multiple_of(head * width, width), width)


def scan_kernel(
    sizes, scale,
    q_hbm, k_hbm, v_hbm, g_hbm, pos_hbm,
    attended_ref, query_grad_ref, key_grad_ref, value_grad_ref,
    q_ref, k_ref, v_ref, g_ref, pos_ref, cos_ref, sin_ref, qrot, krot, partial, before, after,
    theirs, own, pin, chip, xin, row, yin, plane, zin, yout, ybase, xout, xbase, pout, pbase,
    in_s, core_s, core_r, x_s, x_r, y_s, y_r, z_s, z_r, yb_s, yb_r, xb_s, xb_r, cb_s, cb_r,
):
    nx, ny, nz, per = sizes
    inner, outer = (lax.axis_index("inner"), lax.axis_index("outer"))
    x, z = (lax.div(inner, CORES), lax.div(outer, ny))
    c, y = (inner - x * CORES, outer - z * ny)
    tall = D_HEAD // HALVES
    part = tall // ny
    other = 1 - c
    tokens = q_ref.shape[0]

    def at(xx, cc, yy, zz):
        return {"inner": xx * CORES + cc, "outer": zz * ny + yy}

    def shifted(place, by, count):
        return place + by - jnp.where(place + by >= count, count, 0) if by else place

    partner = at(x, other, y, z)
    x_dev = [at(shifted(x, d, nx), c, y, z) for d in range(nx)]
    y_dev = [at(x, c, shifted(y, d, ny), z) for d in range(ny)]
    z_dev = [at(x, c, y, shifted(z, d, nz)) for d in range(nz)]
    arrays = ((pos_hbm, pos_ref), (k_hbm, k_ref), (v_hbm, v_ref), (q_hbm, q_ref), (g_hbm, g_ref))
    fetched = [pltpu.make_async_copy(src, dst, in_s.at[n]) for n, (src, dst) in enumerate(arrays)]
    for copy in fetched:
        copy.start()
    barrier = pltpu.get_barrier_semaphore()
    peers = [partner] + x_dev[1:] + y_dev[1:] + z_dev[1:]
    for peer in peers:
        pl.semaphore_signal(barrier, inc=1, device_id=peer, device_id_type=pl.DeviceIdType.MESH)

    far_first = sorted(range(nx), key=lambda d: (d == 0, -min(d, nx - d)))
    near_first = far_first[::-1]
    sent = []

    def remote(src, dst, send, recv, device):
        return pltpu.make_async_remote_copy(
            src_ref=src, dst_ref=dst, send_sem=send, recv_sem=recv,
            device_id=device, device_id_type=pl.DeviceIdType.MESH,
        )

    def post(*args):
        copy = remote(*args)
        copy.start()
        sent.append(copy)

    fetched[0].wait()
    half = D_HEAD // 2
    pair = lax.broadcasted_iota(jnp.int32, (half, tokens), 0).astype(F32)
    angle = pos_ref[...].astype(F32) * jnp.exp(pair * (-2.0 * math.log(500000.0) / D_HEAD))
    cosine, sine = (jnp.cos(angle), jnp.sin(angle))
    cos_ref[...] = jnp.concatenate([cosine, cosine], axis=0).T
    sin_ref[...] = jnp.concatenate([-sine, sine], axis=0).T

    def head_of(xx, cc, j):
        return (xx * CORES + cc) * per + j

    def states(head, put):
        cols = columns(head)
        cosine, sine = (cos_ref[...], sin_ref[...])
        key = rotate(k_ref[:, cols], cosine, sine).astype(BF16)
        krot[:, cols] = key
        put[0] = dot(key, v_ref[:, cols], 0, 0)
        query = rotate(q_ref[:, cols], cosine, sine).astype(BF16)
        qrot[:, cols] = query
        put[1] = dot(query, g_ref[:, cols], 0, 0)

    def in_block(head):
        cols = columns(head)
        query, key, value, grad = (qrot[:, cols], krot[:, cols], v_ref[:, cols], g_ref[:, cols])
        causal = lax.broadcasted_iota(jnp.int32, (tokens, tokens), 0) >= lax.broadcasted_iota(
            jnp.int32, (tokens, tokens), 1
        )
        scores = jnp.where(causal, dot(query, key, 1, 1), 0.0).astype(BF16)
        grad_scores = jnp.where(causal, dot(grad, value, 1, 1), 0.0).astype(BF16)
        partial[0, :, cols] = dot(scores, value, 1, 0)
        partial[1, :, cols] = dot(grad_scores, key, 1, 0)
        partial[2, :, cols] = dot(grad_scores, query, 0, 0)
        partial[3, :, cols] = dot(scores, grad, 0, 0)

    def finish(head):
        cols = columns(head)
        cosine, sine = (cos_ref[...], sin_ref[...])
        first, last = (before[head], after[head])
        attended = partial[0, :, cols] + dot(qrot[:, cols], first, 1, 0)
        attended_ref[:, cols] = (scale * attended).astype(BF16)
        query_grad = scale * (partial[1, :, cols] + dot(g_ref[:, cols], first, 1, 1))
        query_grad_ref[:, cols] = unrotate(query_grad, cosine, sine).astype(BF16)
        key_grad = scale * (partial[2, :, cols] + dot(v_ref[:, cols], last, 1, 1))
        key_grad_ref[:, cols] = unrotate(key_grad, cosine, sine).astype(BF16)
        value_grad = scale * (partial[3, :, cols] + dot(krot[:, cols], last, 1, 0))
        value_grad_ref[:, cols] = value_grad.astype(BF16)

    def spans(n):
        return n // HALVES, pl.ds((n % HALVES) * tall, tall)

    def send_core(d, j):
        xx = shifted(x, d, nx)
        states(head_of(xx, other, j), theirs.at[xx, j])
        if j == 0 and d == far_first[0]:
            pl.semaphore_wait(barrier, len(peers))
        post(theirs.at[xx, j], pin.at[xx, j], core_s.at[d, j], core_r.at[d, j], partner)

    def keep_own(d, j):
        xx = shifted(x, d, nx)
        states(head_of(xx, c, j), own.at[xx, j])

    def send_x(d, n):
        j, rows = spans(n)
        xx = shifted(x, d, nx)
        if n % HALVES == 0:
            remote(theirs.at[xx, j], pin.at[xx, j], core_s.at[d, j], core_r.at[d, j], partner).wait_recv()
        if d:
            chip[xx, n] = own[xx, j, :, rows] + pin[xx, j, :, rows]
            post(chip.at[xx, n], xin.at[x, n], x_s.at[d, n], x_r.at[d, n], x_dev[d])
        else:
            xin[x, n] = own[x, j, :, rows] + pin[x, j, :, rows]

    def got_x(n):
        for d in range(1, nx):
            src = shifted(x, nx - d, nx)
            remote(chip.at[src, n], xin.at[src, n], x_s.at[d, n], x_r.at[d, n], x_dev[d]).wait_recv()
        total = xin[0, n]
        for xx in range(1, nx):
            total = total + xin[xx, n]
        for yy in range(ny):
            row[n, yy] = total[:, yy * part : (yy + 1) * part]
        for d in sorted(range(1, ny), key=lambda d: -min(d, ny - d)):
            post(row.at[n, shifted(y, d, ny)], yin.at[y, n], y_s.at[d, n], y_r.at[d, n], y_dev[d])
        yin[y, n] = row[n, y]

    def got_y(n):
        for d in range(1, ny):
            src = shifted(y, ny - d, ny)
            remote(yout.at[src, n], yin.at[src, n], y_s.at[d, n], y_r.at[d, n], y_dev[d]).wait_recv()
        total = yin[0, n]
        for yy in range(1, ny):
            total = total + yin[yy, n]
        plane[n] = total
        for d in sorted(range(1, nz), key=lambda d: -min(d, nz - d)):
            which = jnp.where(z + d >= nz, 1, 0)
            post(plane.at[n, which], zin.at[z, n], z_s.at[d, n], z_r.at[d, n], z_dev[d])
        zin[z, n] = jnp.zeros((part, D_HEAD), F32)

    def got_z(n):
        for d in range(1, nz):
            src = shifted(z, nz - d, nz)
            remote(plane.at[n, 0], zin.at[src, n], z_s.at[d, n], z_r.at[d, n], z_dev[d]).wait_recv()
        earlier = jnp.zeros((part, D_HEAD), F32)
        later = jnp.zeros((part, D_HEAD), F32)
        for zz in range(nz):
            piece = zin[zz, n]
            earlier = earlier + jnp.where(zz < z, piece, 0.0)
            later = later + jnp.where(zz > z, piece, 0.0)
        for yy in range(ny):
            yout[yy, n, 0] = earlier
            earlier = earlier + yin[yy, n, 0]
        for yy in reversed(range(ny)):
            yout[yy, n, 1] = later
            later = later + yin[yy, n, 1]
        for d in sorted(range(1, ny), key=lambda d: -min(d, ny - d)):
            post(yout.at[shifted(y, d, ny), n], ybase.at[n, y], yb_s.at[d, n], yb_r.at[d, n], y_dev[d])
        ybase[n, y] = yout[y, n]

    def got_yb(n):
        for d in range(1, ny):
            src = shifted(y, ny - d, ny)
            remote(yout.at[src, n], ybase.at[n, src], yb_s.at[d, n], yb_r.at[d, n], y_dev[d]).wait_recv()
        for cut in range(ny):
            rows = pl.ds(cut * part, part)
            earlier = ybase[n, cut, 0]
            for xx in range(nx):
                xout[xx, n, 0, rows] = earlier
                earlier = earlier + xin[xx, n, 0, rows]
            later = ybase[n, cut, 1]
            for xx in reversed(range(nx)):
                xout[xx, n, 1, rows] = later
                later = later + xin[xx, n, 1, rows]
        for d in far_first[:-1]:
            xx = shifted(x, d, nx)
            post(xout.at[xx, n], xbase.at[x, n], xb_s.at[d, n], xb_r.at[d, n], x_dev[d])
        xbase[x, n] = xout[x, n]

    def got_xb(n):
        j, rows = spans(n)
        for d in near_first:
            src = shifted(x, nx - d, nx)
            if d:
                remote(xout.at[src, n], xbase.at[src, n], xb_s.at[d, n], xb_r.at[d, n], x_dev[d]).wait_recv()
            keys, queries = (xbase[src, n, 0], xbase[src, n, 1])
            pout[src, n, 0] = keys + jnp.where(c == 0, own[src, j, 0, rows], 0.0)
            pout[src, n, 1] = queries + jnp.where(c == 1, own[src, j, 1, rows], 0.0)
            post(pout.at[src, n], pbase.at[src, n], cb_s.at[d, n], cb_r.at[d, n], partner)
            head = head_of(src, c, j)
            before[head, rows] = (keys + jnp.where(c == 1, pin[src, j, 0, rows], 0.0)).astype(BF16)
            after[head, rows] = (queries + jnp.where(c == 0, pin[src, j, 1, rows], 0.0)).astype(BF16)

    def got_cb(n):
        j, rows = spans(n)
        for d in near_first:
            src = shifted(x, nx - d, nx)
            remote(pout.at[src, n], pbase.at[src, n], cb_s.at[d, n], cb_r.at[d, n], partner).wait_recv()
            head = head_of(src, other, j)
            before[head, rows] = pbase[src, n, 0].astype(BF16)
            after[head, rows] = pbase[src, n, 1].astype(BF16)

    def finish_side(j, cc):
        for d in near_first:
            finish(head_of(shifted(x, nx - d, nx), cc, j))

    heads = iter(range(nx * CORES * per))

    def some_heads(count):
        for _ in range(count):
            head = next(heads, None)
            if head is not None:
                in_block(head)

    chunks = per * HALVES
    for copy in fetched[1:]:
        copy.wait()
    for j in range(per):
        for d in far_first:
            send_core(d, j)
        for d in far_first:
            keep_own(d, j)
        for n in range(j * HALVES, (j + 1) * HALVES):
            for d in far_first:
                send_x(d, n)
    some_heads(16)
    stages = ((got_x, 0.0), (got_y, 3.0), (got_z, 8.0), (got_yb, 11.3), (got_xb, 100))
    events = sorted(
        (lag + 9.6 / chunks * n, k, n) for k, (_, lag) in enumerate(stages) for n in range(chunks)
    )
    for _, k, n in events:
        stages[k][0](n)
        if k == 0:
            some_heads(0)
        if k == 4 and n % HALVES == HALVES - 1:
            j = n // HALVES
            some_heads(nx * CORES * per)
            finish_side(j, c)
            for m in range(j * HALVES, n + 1):
                got_cb(m)
            finish_side(j, other)
    for copy in sent:
        copy.wait_send()


def write_kernel(*refs):
    count = len(refs) // 2
    sem = refs[-1]
    copies = [pltpu.make_async_copy(refs[n], refs[count + n], sem.at[n]) for n in range(count)]
    for copy in copies:
        copy.start()
    for copy in copies:
        copy.wait()


def shards(sizes, queries, keys, values, out_grad, positions):
    nx, ny, nz, per = sizes
    tokens, width = queries.shape
    heads = width // D_HEAD
    total_tokens = tokens * lax.axis_size("inner") * lax.axis_size("outer")
    scale = (D_HEAD * total_tokens) ** (-0.5)
    chunks = per * HALVES
    tall = D_HEAD // HALVES
    part = tall // ny

    tokens_bf16 = pltpu.VMEM((tokens, width), BF16)
    table = pltpu.VMEM((tokens, D_HEAD), F32)
    state = pltpu.VMEM((heads, D_HEAD, D_HEAD), BF16)
    by_x = pltpu.VMEM((nx, per, 2, D_HEAD, D_HEAD), F32)
    by_x_chunk = pltpu.VMEM((nx, chunks, 2, tall, D_HEAD), F32)
    by_y = pltpu.VMEM((ny, chunks, 2, part, D_HEAD), F32)
    mine = pltpu.VMEM((chunks, ny, 2, part, D_HEAD), F32)
    in_vmem = pl.BlockSpec(memory_space=pltpu.VMEM)
    in_hbm = pl.BlockSpec(memory_space=pltpu.HBM)
    sems = [pltpu.SemaphoreType.DMA((5,))]
    for count in ((nx, per), (nx, chunks), (ny, chunks), (nz, chunks), (ny, chunks), (nx, chunks), (nx, chunks)):
        sems += [pltpu.SemaphoreType.DMA(count)] * 2
    results = [jax.ShapeDtypeStruct((tokens, width), BF16)] * 4
    arrays = (queries, keys, values, out_grad, positions.reshape(1, tokens))
    arrays = [pltpu.with_memory_space_constraint(a, pltpu.HBM) for a in arrays]
    outputs = pl.pallas_call(
        functools.partial(scan_kernel, sizes, scale),
        out_shape=[pltpu.VMEM((tokens, width), BF16)] * 4,
        in_specs=[in_hbm] * 5,
        out_specs=[in_vmem] * 4,
        scratch_shapes=[tokens_bf16] * 4 + [pltpu.VMEM((1, tokens), jnp.int32)] + [table] * 2 + [tokens_bf16] * 2
        + [pltpu.VMEM((4, tokens, width), F32), state, state]
        + [by_x] * 3 + [by_x_chunk] * 2 + [mine, by_y]
        + [pltpu.VMEM((chunks, 2, part, D_HEAD), F32), pltpu.VMEM((nz, chunks, part, D_HEAD), F32)]
        + [by_y, mine] + [by_x_chunk] * 4 + sems,
        compiler_params=pltpu.CompilerParams(
            collective_id=0, has_side_effects=True, vmem_limit_bytes=48 * 1024 * 1024
        ),
        name="scan",
    )(*arrays)
    return pl.pallas_call(
        write_kernel,
        out_shape=results,
        in_specs=[in_vmem] * 4,
        out_specs=[in_hbm] * 4,
        scratch_shapes=[pltpu.SemaphoreType.DMA((4,))],
        name="write",
    )(*[pltpu.with_memory_space_constraint(a, pltpu.VMEM) for a in outputs])


def solution(mesh):
    inner, outer = (mesh.shape["inner"], mesh.shape["outer"])
    ny = 4 if outer % 16 == 0 else 2
    sizes = (inner // CORES, ny, outer // ny, 16 // inner)
    both = P(("outer", "inner"), None)
    return jax.shard_map(
        functools.partial(shards, sizes),
        mesh=mesh,
        in_specs=(both,) * 4 + (P(("outer", "inner")),),
        out_specs=(both,) * 4,
        check_vma=False,
    )
```

```python
import functools
import math

import jax
import jax.numpy as jnp
from jax import lax
from jax.experimental import pallas as pl
from jax.experimental.pallas import tpu as pltpu
from jax.sharding import PartitionSpec as P

D_HEAD = 128
CORES = 2
HALVES = 2
F32, BF16 = (jnp.float32, jnp.bfloat16)


def rotate(rows, cosine, sine):
    rows = rows.astype(F32)
    return rows * cosine + pltpu.roll(rows, D_HEAD // 2, 1) * sine


def unrotate(rows, cosine, sine):
    return rows * cosine - pltpu.roll(rows, D_HEAD // 2, 1) * sine


def dot(left, right, left_dim, right_dim):
    return lax.dot_general(
        left, right, (((left_dim,), (right_dim,)), ((), ())), preferred_element_type=F32
    )


def columns(head, width=D_HEAD):
    return pl.ds(pl.multiple_of(head * width, width), width)


def scan_kernel(
    sizes, scale,
    q_hbm, k_hbm, v_hbm, g_hbm, pos_hbm,
    attended_ref, query_grad_ref, key_grad_ref, value_grad_ref,
    q_ref, k_ref, v_ref, g_ref, pos_ref, cos_ref, sin_ref, qrot, krot, partial, before, after,
    theirs, own, pin, chip, xin, row, yin, plane, zin, yout, ybase, xout, xbase, pout, pbase,
    in_s, core_s, core_r, x_s, x_r, y_s, y_r, z_s, z_r, yb_s, yb_r, xb_s, xb_r, cb_s, cb_r,
):
    nx, ny, nz, per = sizes
    inner, outer = (lax.axis_index("inner"), lax.axis_index("outer"))
    x, z = (lax.div(inner, CORES), lax.div(outer, ny))
    c, y = (inner - x * CORES, outer - z * ny)
    tall = D_HEAD // HALVES
    part = tall // ny
    other = 1 - c
    tokens = q_ref.shape[0]

    def at(xx, cc, yy, zz):
        return {"inner": xx * CORES + cc, "outer": zz * ny + yy}

    def shifted(place, by, count):
        return place + by - jnp.where(place + by >= count, count, 0) if by else place

    partner = at(x, other, y, z)
    x_dev = [at(shifted(x, d, nx), c, y, z) for d in range(nx)]
    y_dev = [at(x, c, shifted(y, d, ny), z) for d in range(ny)]
    z_dev = [at(x, c, y, shifted(z, d, nz)) for d in range(nz)]
    arrays = ((pos_hbm, pos_ref), (k_hbm, k_ref), (v_hbm, v_ref), (q_hbm, q_ref), (g_hbm, g_ref))
    fetched = [pltpu.make_async_copy(src, dst, in_s.at[n]) for n, (src, dst) in enumerate(arrays)]
    for copy in fetched:
        copy.start()
    barrier = pltpu.get_barrier_semaphore()
    peers = [partner] + x_dev[1:] + y_dev[1:] + z_dev[1:]
    for peer in peers:
        pl.semaphore_signal(barrier, inc=1, device_id=peer, device_id_type=pl.DeviceIdType.MESH)

    far_first = sorted(range(nx), key=lambda d: (d == 0, -min(d, nx - d)))
    near_first = far_first[::-1]
    sent = []

    def remote(src, dst, send, recv, device):
        return pltpu.make_async_remote_copy(
            src_ref=src, dst_ref=dst, send_sem=send, recv_sem=recv,
            device_id=device, device_id_type=pl.DeviceIdType.MESH,
        )

    def post(*args):
        copy = remote(*args)
        copy.start()
        sent.append(copy)

    fetched[0].wait()
    half = D_HEAD // 2
    pair = lax.broadcasted_iota(jnp.int32, (half, tokens), 0).astype(F32)
    angle = pos_ref[...].astype(F32) * jnp.exp(pair * (-2.0 * math.log(500000.0) / D_HEAD))
    cosine, sine = (jnp.cos(angle), jnp.sin(angle))
    cos_ref[...] = jnp.concatenate([cosine, cosine], axis=0).T
    sin_ref[...] = jnp.concatenate([-sine, sine], axis=0).T

    def head_of(xx, cc, j):
        return (xx * CORES + cc) * per + j

    def states(head, put):
        cols = columns(head)
        cosine, sine = (cos_ref[...], sin_ref[...])
        key = rotate(k_ref[:, cols], cosine, sine).astype(BF16)
        krot[:, cols] = key
        put[0] = dot(key, v_ref[:, cols], 0, 0)
        query = rotate(q_ref[:, cols], cosine, sine).astype(BF16)
        qrot[:, cols] = query
        put[1] = dot(query, g_ref[:, cols], 0, 0)

    def in_block(head):
        cols = columns(head)
        query, key, value, grad = (qrot[:, cols], krot[:, cols], v_ref[:, cols], g_ref[:, cols])
        causal = lax.broadcasted_iota(jnp.int32, (tokens, tokens), 0) >= lax.broadcasted_iota(
            jnp.int32, (tokens, tokens), 1
        )
        scores = jnp.where(causal, dot(query, key, 1, 1), 0.0).astype(BF16)
        grad_scores = jnp.where(causal, dot(grad, value, 1, 1), 0.0).astype(BF16)
        partial[0, :, cols] = dot(scores, value, 1, 0)
        partial[1, :, cols] = dot(grad_scores, key, 1, 0)
        partial[2, :, cols] = dot(grad_scores, query, 0, 0)
        partial[3, :, cols] = dot(scores, grad, 0, 0)

    def finish(head):
        cols = columns(head)
        cosine, sine = (cos_ref[...], sin_ref[...])
        first, last = (before[head], after[head])
        attended = partial[0, :, cols] + dot(qrot[:, cols], first, 1, 0)
        attended_ref[:, cols] = (scale * attended).astype(BF16)
        query_grad = scale * (partial[1, :, cols] + dot(g_ref[:, cols], first, 1, 1))
        query_grad_ref[:, cols] = unrotate(query_grad, cosine, sine).astype(BF16)
        key_grad = scale * (partial[2, :, cols] + dot(v_ref[:, cols], last, 1, 1))
        key_grad_ref[:, cols] = unrotate(key_grad, cosine, sine).astype(BF16)
        value_grad = scale * (partial[3, :, cols] + dot(krot[:, cols], last, 1, 0))
        value_grad_ref[:, cols] = value_grad.astype(BF16)

    def spans(n):
        return n // HALVES, pl.ds((n % HALVES) * tall, tall)

    def send_core(d, j):
        xx = shifted(x, d, nx)
        states(head_of(xx, other, j), theirs.at[xx, j])
        if j == 0 and d == far_first[0]:
            pl.semaphore_wait(barrier, len(peers))
        post(theirs.at[xx, j], pin.at[xx, j], core_s.at[d, j], core_r.at[d, j], partner)

    def keep_own(d, j):
        xx = shifted(x, d, nx)
        states(head_of(xx, c, j), own.at[xx, j])

    def send_x(d, n):
        j, rows = spans(n)
        xx = shifted(x, d, nx)
        if n % HALVES == 0:
            remote(theirs.at[xx, j], pin.at[xx, j], core_s.at[d, j], core_r.at[d, j], partner).wait_recv()
        if d:
            chip[xx, n] = own[xx, j, :, rows] + pin[xx, j, :, rows]
            post(chip.at[xx, n], xin.at[x, n], x_s.at[d, n], x_r.at[d, n], x_dev[d])
        else:
            xin[x, n] = own[x, j, :, rows] + pin[x, j, :, rows]

    def got_x(n):
        for d in range(1, nx):
            src = shifted(x, nx - d, nx)
            remote(chip.at[src, n], xin.at[src, n], x_s.at[d, n], x_r.at[d, n], x_dev[d]).wait_recv()
        total = xin[0, n]
        for xx in range(1, nx):
            total = total + xin[xx, n]
        for yy in range(ny):
            row[n, yy] = total[:, yy * part : (yy + 1) * part]
        for d in sorted(range(1, ny), key=lambda d: -min(d, ny - d)):
            post(row.at[n, shifted(y, d, ny)], yin.at[y, n], y_s.at[d, n], y_r.at[d, n], y_dev[d])
        yin[y, n] = row[n, y]

    def got_y(n):
        for d in range(1, ny):
            src = shifted(y, ny - d, ny)
            remote(yout.at[src, n], yin.at[src, n], y_s.at[d, n], y_r.at[d, n], y_dev[d]).wait_recv()
        total = yin[0, n]
        for yy in range(1, ny):
            total = total + yin[yy, n]
        plane[n] = total
        for d in sorted(range(1, nz), key=lambda d: -min(d, nz - d)):
            which = jnp.where(z + d >= nz, 1, 0)
            post(plane.at[n, which], zin.at[z, n], z_s.at[d, n], z_r.at[d, n], z_dev[d])
        zin[z, n] = jnp.zeros((part, D_HEAD), F32)

    def got_z(n):
        for d in range(1, nz):
            src = shifted(z, nz - d, nz)
            remote(plane.at[n, 0], zin.at[src, n], z_s.at[d, n], z_r.at[d, n], z_dev[d]).wait_recv()
        earlier = jnp.zeros((part, D_HEAD), F32)
        later = jnp.zeros((part, D_HEAD), F32)
        for zz in range(nz):
            piece = zin[zz, n]
            earlier = earlier + jnp.where(zz < z, piece, 0.0)
            later = later + jnp.where(zz > z, piece, 0.0)
        for yy in range(ny):
            yout[yy, n, 0] = earlier
            earlier = earlier + yin[yy, n, 0]
        for yy in reversed(range(ny)):
            yout[yy, n, 1] = later
            later = later + yin[yy, n, 1]
        for d in sorted(range(1, ny), key=lambda d: -min(d, ny - d)):
            post(yout.at[shifted(y, d, ny), n], ybase.at[n, y], yb_s.at[d, n], yb_r.at[d, n], y_dev[d])
        ybase[n, y] = yout[y, n]

    def got_yb(n):
        for d in range(1, ny):
            src = shifted(y, ny - d, ny)
            remote(yout.at[src, n], ybase.at[n, src], yb_s.at[d, n], yb_r.at[d, n], y_dev[d]).wait_recv()
        for cut in range(ny):
            rows = pl.ds(cut * part, part)
            earlier = ybase[n, cut, 0]
            for xx in range(nx):
                xout[xx, n, 0, rows] = earlier
                earlier = earlier + xin[xx, n, 0, rows]
            later = ybase[n, cut, 1]
            for xx in reversed(range(nx)):
                xout[xx, n, 1, rows] = later
                later = later + xin[xx, n, 1, rows]
        for d in far_first[:-1]:
            xx = shifted(x, d, nx)
            post(xout.at[xx, n], xbase.at[x, n], xb_s.at[d, n], xb_r.at[d, n], x_dev[d])
        xbase[x, n] = xout[x, n]

    def got_xb(n):
        j, rows = spans(n)
        for d in near_first:
            src = shifted(x, nx - d, nx)
            if d:
                remote(xout.at[src, n], xbase.at[src, n], xb_s.at[d, n], xb_r.at[d, n], x_dev[d]).wait_recv()
            keys, queries = (xbase[src, n, 0], xbase[src, n, 1])
            pout[src, n, 0] = keys + jnp.where(c == 0, own[src, j, 0, rows], 0.0)
            pout[src, n, 1] = queries + jnp.where(c == 1, own[src, j, 1, rows], 0.0)
            post(pout.at[src, n], pbase.at[src, n], cb_s.at[d, n], cb_r.at[d, n], partner)
            head = head_of(src, c, j)
            before[head, rows] = (keys + jnp.where(c == 1, pin[src, j, 0, rows], 0.0)).astype(BF16)
            after[head, rows] = (queries + jnp.where(c == 0, pin[src, j, 1, rows], 0.0)).astype(BF16)

    def got_cb(n):
        j, rows = spans(n)
        for d in near_first:
            src = shifted(x, nx - d, nx)
            remote(pout.at[src, n], pbase.at[src, n], cb_s.at[d, n], cb_r.at[d, n], partner).wait_recv()
            head = head_of(src, other, j)
            before[head, rows] = pbase[src, n, 0].astype(BF16)
            after[head, rows] = pbase[src, n, 1].astype(BF16)

    def finish_side(j, cc):
        for d in near_first:
            finish(head_of(shifted(x, nx - d, nx), cc, j))

    heads = iter(range(nx * CORES * per))

    def some_heads(count):
        for _ in range(count):
            head = next(heads, None)
            if head is not None:
                in_block(head)

    chunks = per * HALVES
    for copy in fetched[1:]:
        copy.wait()
    for j in range(per):
        for d in far_first:
            send_core(d, j)
        for d in far_first:
            keep_own(d, j)
        for n in range(j * HALVES, (j + 1) * HALVES):
            for d in far_first:
                send_x(d, n)
    some_heads(6)
    stages = ((got_x, 0.0), (got_y, 3.0), (got_z, 8.0), (got_yb, 11.3), (got_xb, 100))
    events = sorted(
        (lag + 9.6 / chunks * n, k, n) for k, (_, lag) in enumerate(stages) for n in range(chunks)
    )
    for _, k, n in events:
        stages[k][0](n)
        if k == 0:
            some_heads(5)
        if k == 4 and n % HALVES == HALVES - 1:
            j = n // HALVES
            some_heads(nx * CORES * per)
            finish_side(j, c)
            if n < chunks - 1:
                while len(sent) > HALVES * (2 * nx - 1):
                    sent.pop(0).wait_send()
            for m in range(j * HALVES, n + 1):
                got_cb(m)
            finish_side(j, other)
    for copy in sent:
        copy.wait_send()


def write_kernel(*refs):
    count = len(refs) // 2
    sem = refs[-1]
    copies = [pltpu.make_async_copy(refs[n], refs[count + n], sem.at[n]) for n in range(count)]
    for copy in copies:
        copy.start()
    for copy in copies:
        copy.wait()


def shards(sizes, queries, keys, values, out_grad, positions):
    nx, ny, nz, per = sizes
    tokens, width = queries.shape
    heads = width // D_HEAD
    total_tokens = tokens * lax.axis_size("inner") * lax.axis_size("outer")
    scale = (D_HEAD * total_tokens) ** (-0.5)
    chunks = per * HALVES
    tall = D_HEAD // HALVES
    part = tall // ny

    tokens_bf16 = pltpu.VMEM((tokens, width), BF16)
    table = pltpu.VMEM((tokens, D_HEAD), F32)
    state = pltpu.VMEM((heads, D_HEAD, D_HEAD), BF16)
    by_x = pltpu.VMEM((nx, per, 2, D_HEAD, D_HEAD), F32)
    by_x_chunk = pltpu.VMEM((nx, chunks, 2, tall, D_HEAD), F32)
    by_y = pltpu.VMEM((ny, chunks, 2, part, D_HEAD), F32)
    mine = pltpu.VMEM((chunks, ny, 2, part, D_HEAD), F32)
    in_vmem = pl.BlockSpec(memory_space=pltpu.VMEM)
    in_hbm = pl.BlockSpec(memory_space=pltpu.HBM)
    sems = [pltpu.SemaphoreType.DMA((5,))]
    for count in ((nx, per), (nx, chunks), (ny, chunks), (nz, chunks), (ny, chunks), (nx, chunks), (nx, chunks)):
        sems += [pltpu.SemaphoreType.DMA(count)] * 2
    results = [jax.ShapeDtypeStruct((tokens, width), BF16)] * 4
    arrays = (queries, keys, values, out_grad, positions.reshape(1, tokens))
    arrays = [pltpu.with_memory_space_constraint(a, pltpu.HBM) for a in arrays]
    outputs = pl.pallas_call(
        functools.partial(scan_kernel, sizes, scale),
        out_shape=[pltpu.VMEM((tokens, width), BF16)] * 4,
        in_specs=[in_hbm] * 5,
        out_specs=[in_vmem] * 4,
        scratch_shapes=[tokens_bf16] * 4 + [pltpu.VMEM((1, tokens), jnp.int32)] + [table] * 2 + [tokens_bf16] * 2
        + [pltpu.VMEM((4, tokens, width), F32), state, state]
        + [by_x] * 3 + [by_x_chunk] * 2 + [mine, by_y]
        + [pltpu.VMEM((chunks, 2, part, D_HEAD), F32), pltpu.VMEM((nz, chunks, part, D_HEAD), F32)]
        + [by_y, mine] + [by_x_chunk] * 4 + sems,
        compiler_params=pltpu.CompilerParams(
            collective_id=0, has_side_effects=True, vmem_limit_bytes=48 * 1024 * 1024
        ),
        name="scan",
    )(*arrays)
    return pl.pallas_call(
        write_kernel,
        out_shape=results,
        in_specs=[in_vmem] * 4,
        out_specs=[in_hbm] * 4,
        scratch_shapes=[pltpu.SemaphoreType.DMA((4,))],
        name="write",
    )(*[pltpu.with_memory_space_constraint(a, pltpu.VMEM) for a in outputs])


def solution(mesh):
    inner, outer = (mesh.shape["inner"], mesh.shape["outer"])
    ny = 4 if outer % 16 == 0 else 2
    sizes = (inner // CORES, ny, outer // ny, 16 // inner)
    both = P(("outer", "inner"), None)
    return jax.shard_map(
        functools.partial(shards, sizes),
        mesh=mesh,
        in_specs=(both,) * 4 + (P(("outer", "inner")),),
        out_specs=(both,) * 4,
        check_vma=False,
    )
```

```python
import functools
import math

import jax
import jax.numpy as jnp
from jax import lax
from jax.experimental import pallas as pl
from jax.experimental.pallas import tpu as pltpu
from jax.sharding import PartitionSpec as P

D_HEAD = 128
CORES = 2
HALVES = 2
F32, BF16 = (jnp.float32, jnp.bfloat16)


def rotate(rows, cosine, sine):
    rows = rows.astype(F32)
    return rows * cosine + pltpu.roll(rows, D_HEAD // 2, 1) * sine


def unrotate(rows, cosine, sine):
    return rows * cosine - pltpu.roll(rows, D_HEAD // 2, 1) * sine


def dot(left, right, left_dim, right_dim):
    return lax.dot_general(
        left, right, (((left_dim,), (right_dim,)), ((), ())), preferred_element_type=F32
    )


def columns(head, width=D_HEAD):
    return pl.ds(pl.multiple_of(head * width, width), width)


def scan_kernel(
    sizes, scale,
    q_hbm, k_hbm, v_hbm, g_hbm, pos_hbm,
    attended_ref, query_grad_ref, key_grad_ref, value_grad_ref,
    q_ref, k_ref, v_ref, g_ref, pos_ref, cos_ref, sin_ref, qrot, krot, partial, before, after,
    theirs, own, pin, chip, xin, row, yin, plane, zin, yout, ybase, xout, xbase, pout, pbase,
    in_s, core_s, core_r, x_s, x_r, y_s, y_r, z_s, z_r, yb_s, yb_r, xb_s, xb_r, cb_s, cb_r,
):
    nx, ny, nz, per = sizes
    inner, outer = (lax.axis_index("inner"), lax.axis_index("outer"))
    x, z = (lax.div(inner, CORES), lax.div(outer, ny))
    c, y = (inner - x * CORES, outer - z * ny)
    tall = D_HEAD // HALVES
    part = tall // ny
    other = 1 - c
    tokens = q_ref.shape[0]

    def at(xx, cc, yy, zz):
        return {"inner": xx * CORES + cc, "outer": zz * ny + yy}

    def shifted(place, by, count):
        return place + by - jnp.where(place + by >= count, count, 0) if by else place

    partner = at(x, other, y, z)
    x_dev = [at(shifted(x, d, nx), c, y, z) for d in range(nx)]
    y_dev = [at(x, c, shifted(y, d, ny), z) for d in range(ny)]
    z_dev = [at(x, c, y, shifted(z, d, nz)) for d in range(nz)]
    arrays = ((pos_hbm, pos_ref), (k_hbm, k_ref), (v_hbm, v_ref), (q_hbm, q_ref), (g_hbm, g_ref))
    fetched = [pltpu.make_async_copy(src, dst, in_s.at[n]) for n, (src, dst) in enumerate(arrays)]
    for copy in fetched:
        copy.start()
    barrier = pltpu.get_barrier_semaphore()
    peers = [partner] + x_dev[1:] + y_dev[1:] + z_dev[1:]
    for peer in peers:
        pl.semaphore_signal(barrier, inc=1, device_id=peer, device_id_type=pl.DeviceIdType.MESH)

    far_first = sorted(range(nx), key=lambda d: (d == 0, -min(d, nx - d)))
    near_first = far_first[::-1]
    sent = []

    def remote(src, dst, send, recv, device):
        return pltpu.make_async_remote_copy(
            src_ref=src, dst_ref=dst, send_sem=send, recv_sem=recv,
            device_id=device, device_id_type=pl.DeviceIdType.MESH,
        )

    def post(*args):
        copy = remote(*args)
        copy.start()
        sent.append(copy)

    fetched[0].wait()
    half = D_HEAD // 2
    pair = lax.broadcasted_iota(jnp.int32, (half, tokens), 0).astype(F32)
    angle = pos_ref[...].astype(F32) * jnp.exp(pair * (-2.0 * math.log(500000.0) / D_HEAD))
    cosine, sine = (jnp.cos(angle), jnp.sin(angle))
    cos_ref[...] = jnp.concatenate([cosine, cosine], axis=0).T
    sin_ref[...] = jnp.concatenate([-sine, sine], axis=0).T

    def head_of(xx, cc, j):
        return (xx * CORES + cc) * per + j

    def states(head, put):
        cols = columns(head)
        cosine, sine = (cos_ref[...], sin_ref[...])
        key = rotate(k_ref[:, cols], cosine, sine).astype(BF16)
        krot[:, cols] = key
        put[0] = dot(key, v_ref[:, cols], 0, 0)
        query = rotate(q_ref[:, cols], cosine, sine).astype(BF16)
        qrot[:, cols] = query
        put[1] = dot(query, g_ref[:, cols], 0, 0)

    def in_block(head):
        cols = columns(head)
        query, key, value, grad = (qrot[:, cols], krot[:, cols], v_ref[:, cols], g_ref[:, cols])
        causal = lax.broadcasted_iota(jnp.int32, (tokens, tokens), 0) >= lax.broadcasted_iota(
            jnp.int32, (tokens, tokens), 1
        )
        scores = jnp.where(causal, dot(query, key, 1, 1), 0.0).astype(BF16)
        grad_scores = jnp.where(causal, dot(grad, value, 1, 1), 0.0).astype(BF16)
        partial[0, :, cols] = dot(scores, value, 1, 0)
        partial[1, :, cols] = dot(grad_scores, key, 1, 0)
        partial[2, :, cols] = dot(grad_scores, query, 0, 0)
        partial[3, :, cols] = dot(scores, grad, 0, 0)

    def finish(head):
        cols = columns(head)
        cosine, sine = (cos_ref[...], sin_ref[...])
        first, last = (before[head], after[head])
        attended = partial[0, :, cols] + dot(qrot[:, cols], first, 1, 0)
        attended_ref[:, cols] = (scale * attended).astype(BF16)
        query_grad = scale * (partial[1, :, cols] + dot(g_ref[:, cols], first, 1, 1))
        query_grad_ref[:, cols] = unrotate(query_grad, cosine, sine).astype(BF16)
        key_grad = scale * (partial[2, :, cols] + dot(v_ref[:, cols], last, 1, 1))
        key_grad_ref[:, cols] = unrotate(key_grad, cosine, sine).astype(BF16)
        value_grad = scale * (partial[3, :, cols] + dot(krot[:, cols], last, 1, 0))
        value_grad_ref[:, cols] = value_grad.astype(BF16)

    def spans(n):
        return n // HALVES, pl.ds((n % HALVES) * tall, tall)

    def send_core(d, j):
        xx = shifted(x, d, nx)
        states(head_of(xx, other, j), theirs.at[xx, j])
        if j == 0 and d == far_first[0]:
            pl.semaphore_wait(barrier, len(peers))
        post(theirs.at[xx, j], pin.at[xx, j], core_s.at[d, j], core_r.at[d, j], partner)

    def keep_own(d, j):
        xx = shifted(x, d, nx)
        states(head_of(xx, c, j), own.at[xx, j])

    def send_x(d, n):
        j, rows = spans(n)
        xx = shifted(x, d, nx)
        if n % HALVES == 0:
            remote(theirs.at[xx, j], pin.at[xx, j], core_s.at[d, j], core_r.at[d, j], partner).wait_recv()
        if d:
            chip[xx, n] = own[xx, j, :, rows] + pin[xx, j, :, rows]
            post(chip.at[xx, n], xin.at[x, n], x_s.at[d, n], x_r.at[d, n], x_dev[d])
        else:
            xin[x, n] = own[x, j, :, rows] + pin[x, j, :, rows]

    def got_x(n):
        for d in range(1, nx):
            src = shifted(x, nx - d, nx)
            remote(chip.at[src, n], xin.at[src, n], x_s.at[d, n], x_r.at[d, n], x_dev[d]).wait_recv()
        total = xin[0, n]
        for xx in range(1, nx):
            total = total + xin[xx, n]
        for yy in range(ny):
            row[n, yy] = total[:, yy * part : (yy + 1) * part]
        for d in sorted(range(1, ny), key=lambda d: -min(d, ny - d)):
            post(row.at[n, shifted(y, d, ny)], yin.at[y, n], y_s.at[d, n], y_r.at[d, n], y_dev[d])
        yin[y, n] = row[n, y]

    def got_y(n):
        for d in range(1, ny):
            src = shifted(y, ny - d, ny)
            remote(yout.at[src, n], yin.at[src, n], y_s.at[d, n], y_r.at[d, n], y_dev[d]).wait_recv()
        total = yin[0, n]
        for yy in range(1, ny):
            total = total + yin[yy, n]
        plane[n] = total
        for d in sorted(range(1, nz), key=lambda d: -min(d, nz - d)):
            which = jnp.where(z + d >= nz, 1, 0)
            post(plane.at[n, which], zin.at[z, n], z_s.at[d, n], z_r.at[d, n], z_dev[d])
        zin[z, n] = jnp.zeros((part, D_HEAD), F32)

    def got_z(n):
        for d in range(1, nz):
            src = shifted(z, nz - d, nz)
            remote(plane.at[n, 0], zin.at[src, n], z_s.at[d, n], z_r.at[d, n], z_dev[d]).wait_recv()
        earlier = jnp.zeros((part, D_HEAD), F32)
        later = jnp.zeros((part, D_HEAD), F32)
        for zz in range(nz):
            piece = zin[zz, n]
            earlier = earlier + jnp.where(zz < z, piece, 0.0)
            later = later + jnp.where(zz > z, piece, 0.0)
        for yy in range(ny):
            yout[yy, n, 0] = earlier
            earlier = earlier + yin[yy, n, 0]
        for yy in reversed(range(ny)):
            yout[yy, n, 1] = later
            later = later + yin[yy, n, 1]
        for d in sorted(range(1, ny), key=lambda d: -min(d, ny - d)):
            post(yout.at[shifted(y, d, ny), n], ybase.at[n, y], yb_s.at[d, n], yb_r.at[d, n], y_dev[d])
        ybase[n, y] = yout[y, n]

    def got_yb(n):
        for d in range(1, ny):
            src = shifted(y, ny - d, ny)
            remote(yout.at[src, n], ybase.at[n, src], yb_s.at[d, n], yb_r.at[d, n], y_dev[d]).wait_recv()
        for cut in range(ny):
            rows = pl.ds(cut * part, part)
            earlier = ybase[n, cut, 0]
            for xx in range(nx):
                xout[xx, n, 0, rows] = earlier
                earlier = earlier + xin[xx, n, 0, rows]
            later = ybase[n, cut, 1]
            for xx in reversed(range(nx)):
                xout[xx, n, 1, rows] = later
                later = later + xin[xx, n, 1, rows]
        for d in far_first[:-1]:
            xx = shifted(x, d, nx)
            post(xout.at[xx, n], xbase.at[x, n], xb_s.at[d, n], xb_r.at[d, n], x_dev[d])
        xbase[x, n] = xout[x, n]

    def got_xb(n):
        j, rows = spans(n)
        for d in near_first:
            src = shifted(x, nx - d, nx)
            if d:
                remote(xout.at[src, n], xbase.at[src, n], xb_s.at[d, n], xb_r.at[d, n], x_dev[d]).wait_recv()
            keys, queries = (xbase[src, n, 0], xbase[src, n, 1])
            pout[src, n, 0] = keys + jnp.where(c == 0, own[src, j, 0, rows], 0.0)
            pout[src, n, 1] = queries + jnp.where(c == 1, own[src, j, 1, rows], 0.0)
            post(pout.at[src, n], pbase.at[src, n], cb_s.at[d, n], cb_r.at[d, n], partner)
            head = head_of(src, c, j)
            before[head, rows] = (keys + jnp.where(c == 1, pin[src, j, 0, rows], 0.0)).astype(BF16)
            after[head, rows] = (queries + jnp.where(c == 0, pin[src, j, 1, rows], 0.0)).astype(BF16)

    def got_cb(n):
        j, rows = spans(n)
        for d in near_first:
            src = shifted(x, nx - d, nx)
            remote(pout.at[src, n], pbase.at[src, n], cb_s.at[d, n], cb_r.at[d, n], partner).wait_recv()
            head = head_of(src, other, j)
            before[head, rows] = pbase[src, n, 0].astype(BF16)
            after[head, rows] = pbase[src, n, 1].astype(BF16)

    def finish_side(j, cc):
        for d in near_first:
            finish(head_of(shifted(x, nx - d, nx), cc, j))

    heads = iter(range(nx * CORES * per))

    def some_heads(count):
        for _ in range(count):
            head = next(heads, None)
            if head is not None:
                in_block(head)

    chunks = per * HALVES
    for copy in fetched[1:]:
        copy.wait()
    for j in range(per):
        for d in far_first:
            send_core(d, j)
        for d in far_first:
            keep_own(d, j)
        for n in range(j * HALVES, (j + 1) * HALVES):
            for d in far_first:
                send_x(d, n)
    some_heads(6)
    stages = (got_x, got_y, got_z, got_yb, got_xb)
    events = [(0.0, 0, 0), (0.0, 0, 1), (0.0, 1, 0), (0.0, 0, 2), (0.0, 1, 1), (0.0, 0, 3), (0.0, 2, 0), (0.0, 1, 2), (0.0, 1, 3), (0.0, 3, 0), (0.0, 2, 1), (0.0, 2, 2), (0.0, 3, 1), (0.0, 2, 3), (0.0, 3, 2), (0.0, 3, 3), (0.0, 4, 0), (0.0, 4, 1), (0.0, 4, 2), (0.0, 4, 3)]
    for _, k, n in events:
        stages[k](n)
        if k == 0:
            some_heads(5)
        if k == 4 and n % HALVES == HALVES - 1:
            j = n // HALVES
            some_heads(nx * CORES * per)
            finish_side(j, c)
            if n < chunks - 1:
                while len(sent) > HALVES * (2 * nx - 1):
                    sent.pop(0).wait_send()
            for m in range(j * HALVES, n + 1):
                got_cb(m)
            finish_side(j, other)
    for copy in sent:
        copy.wait_send()


def write_kernel(*refs):
    count = len(refs) // 2
    sem = refs[-1]
    copies = [pltpu.make_async_copy(refs[n], refs[count + n], sem.at[n]) for n in range(count)]
    for copy in copies:
        copy.start()
    for copy in copies:
        copy.wait()


def shards(sizes, queries, keys, values, out_grad, positions):
    nx, ny, nz, per = sizes
    tokens, width = queries.shape
    heads = width // D_HEAD
    total_tokens = tokens * lax.axis_size("inner") * lax.axis_size("outer")
    scale = (D_HEAD * total_tokens) ** (-0.5)
    chunks = per * HALVES
    tall = D_HEAD // HALVES
    part = tall // ny

    tokens_bf16 = pltpu.VMEM((tokens, width), BF16)
    table = pltpu.VMEM((tokens, D_HEAD), F32)
    state = pltpu.VMEM((heads, D_HEAD, D_HEAD), BF16)
    by_x = pltpu.VMEM((nx, per, 2, D_HEAD, D_HEAD), F32)
    by_x_chunk = pltpu.VMEM((nx, chunks, 2, tall, D_HEAD), F32)
    by_y = pltpu.VMEM((ny, chunks, 2, part, D_HEAD), F32)
    mine = pltpu.VMEM((chunks, ny, 2, part, D_HEAD), F32)
    in_vmem = pl.BlockSpec(memory_space=pltpu.VMEM)
    in_hbm = pl.BlockSpec(memory_space=pltpu.HBM)
    sems = [pltpu.SemaphoreType.DMA((5,))]
    for count in ((nx, per), (nx, chunks), (ny, chunks), (nz, chunks), (ny, chunks), (nx, chunks), (nx, chunks)):
        sems += [pltpu.SemaphoreType.DMA(count)] * 2
    results = [jax.ShapeDtypeStruct((tokens, width), BF16)] * 4
    arrays = (queries, keys, values, out_grad, positions.reshape(1, tokens))
    arrays = [pltpu.with_memory_space_constraint(a, pltpu.HBM) for a in arrays]
    outputs = pl.pallas_call(
        functools.partial(scan_kernel, sizes, scale),
        out_shape=[pltpu.VMEM((tokens, width), BF16)] * 4,
        in_specs=[in_hbm] * 5,
        out_specs=[in_vmem] * 4,
        scratch_shapes=[tokens_bf16] * 4 + [pltpu.VMEM((1, tokens), jnp.int32)] + [table] * 2 + [tokens_bf16] * 2
        + [pltpu.VMEM((4, tokens, width), F32), state, state]
        + [by_x] * 3 + [by_x_chunk] * 2 + [mine, by_y]
        + [pltpu.VMEM((chunks, 2, part, D_HEAD), F32), pltpu.VMEM((nz, chunks, part, D_HEAD), F32)]
        + [by_y, mine] + [by_x_chunk] * 4 + sems,
        compiler_params=pltpu.CompilerParams(
            collective_id=0, has_side_effects=True, vmem_limit_bytes=48 * 1024 * 1024
        ),
        name="scan",
    )(*arrays)
    return pl.pallas_call(
        write_kernel,
        out_shape=results,
        in_specs=[in_vmem] * 4,
        out_specs=[in_hbm] * 4,
        scratch_shapes=[pltpu.SemaphoreType.DMA((4,))],
        name="write",
    )(*[pltpu.with_memory_space_constraint(a, pltpu.VMEM) for a in outputs])


def solution(mesh):
    inner, outer = (mesh.shape["inner"], mesh.shape["outer"])
    ny = 4 if outer % 16 == 0 else 2
    sizes = (inner // CORES, ny, outer // ny, 16 // inner)
    both = P(("outer", "inner"), None)
    return jax.shard_map(
        functools.partial(shards, sizes),
        mesh=mesh,
        in_specs=(both,) * 4 + (P(("outer", "inner")),),
        out_specs=(both,) * 4,
        check_vma=False,
    )
```
